512 devices in a mesh: tmpl: 64 (over z, y_hi, core), dom: 8 (over y_lo, x).
Axes of the slice: x: 4, y: 4 (y_hi: 2, y_lo: 2; y = y_hi * 2 + y_lo), z: 16, core: 2. Of those that a mesh axis runs over, the one named last changes fastest.
Arguments:
- particles: bfloat16 [8192, 16384], P('tmpl', 'dom'), may hold values from -8 to 8
- templates: bfloat16 [128, 18, 16384], P('tmpl', None, 'dom')
- classes: int32 [8192, 1], P('tmpl'), may hold values from 0 to 127; in each aligned block of 128 rows (0 to 127, 128 to 255, ...) at most 2 rows name the same one
- rotations: int32 [8192], P('tmpl'), may hold values from 0 to 17
Outputs:
- class_means: float32 [128, 18, 16384], P('tmpl', None, 'dom')
- weights: bfloat16 [8192], P('tmpl')
The draws below stay inside these ranges and needn't reach their ends.
Inputs may be any that keep to these rules, and one draw needn't show every extreme that they name: `classes`: among the 128 particles of one index of tmpl (aligned blocks of rows) no class appears more than 2 times, and some class appears exactly 2 times.
All inputs are finite; a program needn't handle non-finite values.
Results may differ from the reference program's by a relative error of at most 0.0022.
Values may be sent and summed in bfloat16 or wider, within the bound.
No kernel may reach another device: no remote copies, remote signals or barrier semaphores. Data moves between devices by JAX's collectives and lax.ppermute only.
A program may use at most 64 MiB of HBM per device.

```python
import math
import jax
import jax.numpy as jnp
import numpy as np
from jax import lax

CLASSES = 128
ROTATIONS = 18
PIXELS = 16384
PART_DEV = 128
CAPACITY = 2
PARTICLES = 8192
N_TMPL = 64


def template_fields(key):
    base_key = jax.random.fold_in(key, 11)
    noise_key, scale_key = jax.random.split(base_key, 2)
    array_shape = (CLASSES, ROTATIONS, PIXELS)
    noise_field = jax.random.normal(noise_key, array_shape, jnp.float32)
    scales = jnp.exp(jax.random.uniform(scale_key, (CLASSES, ROTATIONS, 1), jnp.float32, 0.0, math.log(10.0)))
    return (noise_field, scales)


def draw_templates(key, part):
    noise_field, scales = template_fields(key)
    return (noise_field * scales / math.sqrt(PIXELS)).astype(jnp.bfloat16)


def draw_particles(key, part):
    noise_field, scales = template_fields(key)
    own_key = jax.random.fold_in(key, 23)
    base_key, source_key, strength_key = jax.random.split(own_key, 3)
    array_shape = (PARTICLES, PIXELS)
    background = jax.random.normal(base_key, array_shape, jnp.float32)
    columns = CLASSES * ROTATIONS
    source = jax.random.randint(source_key, (PARTICLES,), 0, columns)
    strength = jax.random.uniform(strength_key, (PARTICLES,), jnp.float32, 0.7, 2.0)
    flat_fields = noise_field.reshape(columns, PIXELS)
    flat_scales = scales.reshape(columns)
    factor = columns * 21.5 / PIXELS
    amplitude = jnp.minimum(jnp.sqrt(factor * strength) / flat_scales[source], 3.0)
    signal = flat_fields[source] * amplitude[:, None]
    return jnp.clip(background + signal, -8.0, 8.0).astype(jnp.bfloat16)


def place_ends(array, stream_key, least, top_value):
    shape = array.shape
    index_at = [jax.random.randint(jax.random.fold_in(stream_key, axis), (), 0, shape[axis]) for axis in range(len(shape))]
    array = array.at[tuple(index_at)].set(least)
    longest = shape.index(max(shape))
    index_at[longest] = (index_at[longest] + 1) % shape[longest]
    return array.at[tuple(index_at)].set(top_value)


def routed_block(key, own, number, rows, amount, top, limit, slope):
    ranking = jax.random.permutation(key, amount)
    crowded, usual = portions_of(amount, rows * top, limit, slope, True), portions_of(amount, rows * top, limit, slope, False)
    places = jnp.arange(amount)

    def named(lengths, rotation):
        used = int((lengths > 0).sum())
        fixed = max(1, used // 4)
        shifted = fixed + (places - fixed + rotation * (used - fixed)) % max(1, amount - fixed)
        return jnp.zeros((amount,), jnp.int32).at[ranking[jnp.where(places < fixed, places, shifted)]].set(jnp.asarray(lengths, jnp.int32))

    lengths = jnp.where(number % 4 == 0, named(crowded, number // 4), named(usual, number - number // 4 - 1))
    mixed = jax.random.permutation(jax.random.fold_in(own, 3), amount)
    donor, receiver = mixed[0:amount // 2 * 2:2], mixed[1:amount // 2 * 2:2]
    room = jnp.minimum(lengths[donor] - 1, limit - lengths[receiver]) // 2
    room = jnp.where((donor == ranking[0]) | (receiver == ranking[0]) | (lengths[receiver] == 0), 0, jnp.maximum(room, 0))
    shifted = jax.random.randint(jax.random.fold_in(own, 4), (amount // 2,), 0, 1 << 20) % (room + 1)
    lengths = lengths.at[donor].add(-shifted).at[receiver].add(shifted)
    labels = jnp.searchsorted(jnp.cumsum(lengths), jnp.arange(rows * top), side="right").astype(jnp.int32)
    grid = labels.reshape(top, rows).T
    grid = grid[jax.random.permutation(jax.random.fold_in(own, 1), rows)]
    rotation = jax.random.randint(jax.random.fold_in(own, 2), (rows, 1), 0, top)
    return jnp.take_along_axis(grid, (jnp.arange(top)[None, :] + rotation) % top, axis=1)


def portions_of(number_of, total, reach, slope, full):
    loads = [(1 << 20) // math.isqrt(rank ** slope) + 1 for rank in range(1, number_of + 1)]
    largest = reach if full else min(reach, max(-(-total // number_of), total * loads[0] // sum(loads)))
    least = 1 if total - largest >= number_of - 1 else 0
    holding, rest = [largest] + [least] * (number_of - 1), total - largest - least * (number_of - 1)
    while rest > 0:
        free = [i for i in range(1, number_of) if holding[i] < largest] or [i for i in range(1, number_of) if holding[i] < reach]
        pool, left = sum([loads[i] for i in free]), rest
        for i in free:
            more = min(reach - holding[i], max(1, left * loads[i] // pool), rest)
            holding[i] = holding[i] + more
            rest = rest - more
    return np.array(holding)


def setup_inputs(seed: int = 0) -> dict:
    seeds = jax.random.split(jax.random.key(seed), 5)
    particles = draw_particles(jax.random.fold_in(seeds[4], 71), 0)
    templates = draw_templates(jax.random.fold_in(seeds[4], 71), 0)
    classes_keys = jax.random.split(jax.random.fold_in(seeds[2], 1), PARTICLES // PART_DEV)
    classes_turns = jax.random.permutation(jax.random.fold_in(seeds[2], 3), PARTICLES // PART_DEV)
    classes = jax.vmap(lambda own, number: routed_block(jax.random.fold_in(seeds[2], 2), own, number, PART_DEV, CLASSES, 1, CAPACITY, 2))(classes_keys, classes_turns).reshape((PARTICLES, 1))
    rotations = place_ends(jax.random.randint(seeds[3], (PARTICLES,), 0, ROTATIONS), jax.random.fold_in(seeds[3], 1), 0, ROTATIONS - 1).astype(jnp.int32)
    return {"particles": particles, "templates": templates, "classes": classes, "rotations": rotations}


eps = 1e-5


def block_weights(particle_block, class_block, rot_block, flat_templates):
    scores = jnp.dot(particle_block.astype(jnp.float32), flat_templates.T, precision=lax.Precision.HIGHEST)
    target = (class_block * ROTATIONS + rot_block).astype(jnp.int32)
    picked = jnp.take_along_axis(scores, target[:, None], axis=1)[:, 0]
    mean_sq = jnp.mean(scores * scores, axis=1)
    return (picked * picked / (mean_sq + eps)).astype(jnp.bfloat16)


def reference(particles, templates, classes, rotations):
    flat_templates = templates.reshape(CLASSES * ROTATIONS, PIXELS).astype(jnp.float32)
    particle_blocks = particles.reshape(N_TMPL, PART_DEV, PIXELS)
    class_blocks = classes[:, 0].reshape(N_TMPL, PART_DEV)
    rot_blocks = rotations.reshape(N_TMPL, PART_DEV)

    def one_block(running, inputs):
        particle_block, class_block, rot_block = inputs
        block_w = block_weights(particle_block, class_block, rot_block, flat_templates)
        target = (class_block * ROTATIONS + rot_block).astype(jnp.int32)
        weight_f = block_w.astype(jnp.float32)
        contrib = jax.ops.segment_sum(weight_f[:, None] * particle_block.astype(jnp.float32), target, num_segments=CLASSES * ROTATIONS)
        total_part = jax.ops.segment_sum(weight_f, target, num_segments=CLASSES * ROTATIONS)
        return (running[0] + contrib, running[1] + total_part), block_w

    initial = (jnp.zeros((CLASSES * ROTATIONS, PIXELS), jnp.float32), jnp.zeros((CLASSES * ROTATIONS,), jnp.float32))
    (class_sums, totals), weights = lax.scan(one_block, initial, (particle_blocks, class_blocks, rot_blocks))
    class_means = class_sums / jnp.maximum(totals, 1.0)[:, None]
    return class_means.reshape(CLASSES, ROTATIONS, PIXELS), weights.reshape(PARTICLES)
```

```python
import jax
import jax.numpy as jnp
from jax import lax
from jax.sharding import PartitionSpec as P

CAPACITY = 2
SLAB = 4
eps = 1e-05


def body(particles, templates, classes, rotations):
    part_rows, pix_width = particles.shape
    local_classes, rot_count, _ = templates.shape
    block_rows = local_classes * rot_count
    owners = lax.axis_size("tmpl")
    doms = lax.axis_size("dom")
    depth = owners // SLAB
    column_count = owners * block_rows
    me = lax.axis_index("tmpl")
    dom_id = lax.axis_index("dom")
    quad = me % SLAB
    core = me % 2
    level = me // SLAB

    def index_of(z, q):
        return (z % depth) * SLAB + q

    everyone = [(z, q) for z in range(depth) for q in range(SLAB)]
    ring = [(index_of(z, q), index_of(z + (1 if q % 2 == 0 else -1), q)) for z, q in everyone]
    core_swap = [(index_of(z, q), index_of(z, q ^ 1)) for z, q in everyone]
    y_swap = [(index_of(z, q), index_of(z, q ^ 2)) for z, q in everyone]

    class_ids = classes[:, 0]
    row_iota = lax.broadcasted_iota(jnp.int32, (part_rows, part_rows), 0)
    col_iota = lax.broadcasted_iota(jnp.int32, (part_rows, part_rows), 1)
    same_class = (class_ids[:, None] == class_ids[None, :]) & (row_iota < col_iota)
    ranks = jnp.sum(same_class.astype(jnp.int32), axis=0)
    slots = class_ids * CAPACITY + ranks
    slot_count = owners * local_classes * CAPACITY

    half = depth // 2
    same_core = [templates]
    for _ in range(half):
        same_core.append(lax.ppermute(same_core[-1], "tmpl", ring))
    other_core = [lax.ppermute(templates, "tmpl", core_swap)]
    for _ in range(half - 1):
        other_core.append(lax.ppermute(other_core[-1], "tmpl", ring))
    blocks = same_core + other_core[1:]

    meta = jnp.stack([slots, rotations]).astype(jnp.bfloat16)
    meta = jnp.pad(meta, ((0, 14), (0, pix_width - part_rows)))
    own = jnp.concatenate([particles, meta], axis=0)
    side = lax.ppermute(own, "tmpl", core_swap)
    across = lax.ppermute(own, "tmpl", y_swap)
    corner = lax.ppermute(across, "tmpl", core_swap)
    quads = [own, side, across, corner]
    slab = jnp.concatenate([b[:part_rows] for b in quads], axis=0)
    slab_slots = jnp.stack([b[part_rows, :part_rows] for b in quads]).astype(jnp.int32)
    slab_rots = jnp.stack([b[part_rows + 1, :part_rows] for b in quads]).astype(jnp.int32)
    slab_target = (slab_slots // CAPACITY * rot_count + slab_rots).reshape(-1)

    slot_iota = lax.broadcasted_iota(jnp.int32, (slot_count, part_rows), 0)
    place = (slot_iota == slots[None, :]).astype(jnp.bfloat16)
    outgoing = jnp.dot(place, particles, preferred_element_type=jnp.float32).astype(jnp.bfloat16)
    per_owner = local_classes * CAPACITY
    outgoing = outgoing.reshape(owners, per_owner, pix_width)
    incoming = lax.all_to_all(outgoing, "tmpl", split_axis=0, concat_axis=0, tiled=True)
    incoming = incoming.reshape(slot_count, pix_width)

    panel = jnp.concatenate(
        [b.transpose(1, 0, 2).reshape(block_rows, pix_width) for b in blocks], axis=0
    )
    scores = lax.dot_general(
        panel, slab, (((1,), (1,)), ((), ())), preferred_element_type=jnp.float32
    )
    panel_rows = panel.shape[0]
    share = panel_rows // doms
    pieces = scores.reshape(doms, share, SLAB * part_rows)
    pieces = lax.all_to_all(pieces, "dom", split_axis=0, concat_axis=0, tiled=True)
    summed = jnp.sum(pieces, axis=0)

    block_id = lax.broadcasted_iota(jnp.int32, (panel_rows,), 0) // block_rows
    inner = lax.broadcasted_iota(jnp.int32, (panel_rows,), 0) % block_rows
    is_other = block_id > half
    hops = jnp.where(is_other, block_id - half, block_id)
    source_core = jnp.where(is_other, 1 - core, core)
    source_z = (level + jnp.where(core == 0, -hops, hops) + depth) % depth
    source = source_z * SLAB + quad // 2 * 2 + source_core
    columns = (source * local_classes + inner % local_classes) * rot_count + inner // local_classes
    my_columns = lax.dynamic_slice(columns, (dom_id * share,), (share,))

    hit = my_columns[:, None] == slab_target[None, :]
    picked = jnp.sum(jnp.where(hit, summed, 0.0), axis=0)
    square = jnp.sum(summed * summed, axis=0)
    vectors = jnp.stack([square, picked]).reshape(2, SLAB, part_rows)

    group = SLAB * doms
    spread = jnp.broadcast_to(vectors[None], (group, 2, SLAB, part_rows))
    groups = [
        [index_of(z, q) * doms + d for q in range(SLAB) for d in range(doms)] for z in range(depth)
    ]
    gathered = lax.all_to_all(
        spread, ("tmpl", "dom"), split_axis=0, concat_axis=0, tiled=True, axis_index_groups=groups
    )
    gathered = jnp.sum(gathered.reshape(SLAB, doms, 2, SLAB, part_rows), axis=1)
    totals4 = jnp.stack(
        [sum(gathered[s, :, s ^ g] for s in range(SLAB)) for g in range(SLAB)], axis=1
    )
    slab_weights = (totals4[1] * totals4[1] / (totals4[0] / column_count + eps)).astype(
        jnp.bfloat16
    )
    quad_iota = lax.broadcasted_iota(jnp.int32, (SLAB, 1), 0)
    weights = jnp.sum(
        jnp.where(quad_iota == quad, slab_weights.astype(jnp.float32), 0.0), axis=0
    ).astype(jnp.bfloat16)

    def canonical(x):
        y = jnp.where(core == 1, x[jnp.array([1, 0, 3, 2])], x)
        return jnp.where(quad >= 2, y[jnp.array([2, 3, 0, 1])], y)

    slots4 = canonical(slab_slots)
    rots4 = canonical(slab_rots)
    z_slots = depth * per_owner
    z_iota = lax.broadcasted_iota(jnp.int32, (1, 1, z_slots), 2)
    wanted = (z_iota // per_owner * SLAB + quad) * per_owner + z_iota % per_owner
    at_slot = (slots4[:, :, None] == wanted).astype(jnp.bfloat16)
    values = jnp.stack([slab_weights, rots4.astype(jnp.bfloat16)], axis=1)
    placed = jnp.einsum(
        "gvn,gns->gvs", values, at_slot, preferred_element_type=jnp.float32
    ).astype(jnp.bfloat16)
    placed = placed.reshape(SLAB, 2, depth, per_owner).transpose(2, 1, 0, 3)
    placed = placed.reshape(depth, 2, SLAB * per_owner)
    z_groups = [[index_of(z, q) for z in range(depth)] for q in range(SLAB)]
    arrived = lax.all_to_all(
        placed, "tmpl", split_axis=0, concat_axis=0, tiled=True, axis_index_groups=z_groups
    )
    slot_weights = arrived[:, 0].reshape(1, slot_count)
    slot_rots = arrived[:, 1].reshape(1, slot_count).astype(jnp.int32)

    row = lax.broadcasted_iota(jnp.int32, (block_rows, slot_count), 0)
    slot = lax.broadcasted_iota(jnp.int32, (block_rows, slot_count), 1)
    match = (row % local_classes == slot % per_owner // CAPACITY) & (
        row // local_classes == slot_rots
    )
    matrix = jnp.where(match, slot_weights, jnp.zeros((), jnp.bfloat16))
    sums = jnp.dot(matrix, incoming, preferred_element_type=jnp.float32)
    totals = jnp.sum(matrix.astype(jnp.float32), axis=1, keepdims=True)
    means = sums / jnp.maximum(totals, 1.0)
    class_means = means.reshape(rot_count, local_classes, pix_width).transpose(1, 0, 2)
    return (class_means, weights)


def solution(mesh):
    return jax.shard_map(
        body,
        mesh=mesh,
        in_specs=(P("tmpl", "dom"), P("tmpl", None, "dom"), P("tmpl", None), P("tmpl")),
        out_specs=(P("tmpl", None, "dom"), P("tmpl")),
        check_vma=False,
    )
```

```python
import jax
import jax.numpy as jnp
from jax import lax
from jax.experimental import pallas as pl
from jax.experimental.pallas import tpu as pltpu
from jax.sharding import PartitionSpec as P

CAPACITY = 2
SLAB = 4
eps = 1e-05


BLOCK_PAD = 48
CHUNK = 4


def correlate_kernel(bundle_sizes, part_rows, *refs):
    bundles = refs[: len(bundle_sizes)]
    quads = refs[len(bundle_sizes) : len(bundle_sizes) + SLAB]
    out, slab, panel = refs[len(bundle_sizes) + SLAB :]
    rows = bundles[0].shape[1]
    blocks = [(ref, i) for ref, size in zip(bundles, bundle_sizes) for i in range(size)]
    for i in range(SLAB):
        slab[part_rows * i : part_rows * (i + 1), :] = quads[i][:part_rows, :]
    pad = jnp.zeros((BLOCK_PAD - rows, slab.shape[1]), jnp.bfloat16)
    for j in range(0, len(blocks), CHUNK):
        for i in range(CHUNK):
            ref, k = blocks[j + i]
            panel[BLOCK_PAD * i : BLOCK_PAD * (i + 1), :] = jnp.concatenate([ref[k], pad], axis=0)
        scores = lax.dot_general(
            panel[...], slab[...], (((1,), (1,)), ((), ())), preferred_element_type=jnp.float32
        )
        kept = [scores[BLOCK_PAD * i : BLOCK_PAD * i + rows] for i in range(CHUNK)]
        out[rows * j : rows * (j + CHUNK), :] = jnp.concatenate(kept, axis=0)


def correlate(bundles, quads, part_rows):
    sizes = [b.shape[0] for b in bundles]
    _, rows, width = bundles[0].shape
    count = sum(sizes)
    vmem = pl.BlockSpec(memory_space=pltpu.VMEM)

    def kernel(*refs):
        correlate_kernel(sizes, part_rows, *refs)

    return pl.pallas_call(
        kernel,
        out_shape=jax.ShapeDtypeStruct((count * rows, SLAB * part_rows), jnp.float32),
        in_specs=[vmem] * (len(sizes) + SLAB),
        out_specs=vmem,
        scratch_shapes=[
            pltpu.VMEM((SLAB * part_rows, width), jnp.bfloat16),
            pltpu.VMEM((CHUNK * BLOCK_PAD, width), jnp.bfloat16),
        ],
        cost_estimate=pl.CostEstimate(
            flops=2 * count * rows * width * SLAB * part_rows,
            bytes_accessed=(count * rows + SLAB * part_rows) * width * 2,
            transcendentals=0,
        ),
        name="correlate",
    )(*bundles, *quads)


def body(particles, templates, classes, rotations):
    part_rows, pix_width = particles.shape
    local_classes, rot_count, _ = templates.shape
    block_rows = local_classes * rot_count
    owners = lax.axis_size("tmpl")
    doms = lax.axis_size("dom")
    depth = owners // SLAB
    column_count = owners * block_rows
    me = lax.axis_index("tmpl")
    dom_id = lax.axis_index("dom")
    quad = me % SLAB
    core = me % 2
    level = me // SLAB

    def index_of(z, q):
        return (z % depth) * SLAB + q

    everyone = [(z, q) for z in range(depth) for q in range(SLAB)]
    core_swap = [(index_of(z, q), index_of(z, q ^ 1)) for z, q in everyone]
    y_swap = [(index_of(z, q), index_of(z, q ^ 2)) for z, q in everyone]

    class_ids = classes[:, 0]
    row_iota = lax.broadcasted_iota(jnp.int32, (part_rows, part_rows), 0)
    col_iota = lax.broadcasted_iota(jnp.int32, (part_rows, part_rows), 1)
    same_class = (class_ids[:, None] == class_ids[None, :]) & (row_iota < col_iota)
    ranks = jnp.sum(same_class.astype(jnp.int32), axis=0)
    slots = class_ids * CAPACITY + ranks
    slot_count = owners * local_classes * CAPACITY

    def along(x, distance):
        hop = [(index_of(z, q), index_of(z + distance, q)) for z, q in everyone]
        return lax.ppermute(x, "tmpl", hop)

    own_block = templates.transpose(1, 0, 2).reshape(1, block_rows, pix_width)
    jump = 5
    trio = jnp.concatenate([own_block, along(own_block, -jump), along(own_block, jump)], axis=0)
    ups, downs = [trio], [trio]
    for _ in range(2):
        ups.append(along(ups[-1], -1))
        downs.append(along(downs[-1], 1))
    last = along(ups[2][1:2], -1)
    bundles = ups + downs[1:] + [last]
    centres = [0, jump, -jump]
    offsets = [c + s for s in (0, 1, 2, -1, -2) for c in centres] + [jump + 3]

    meta = jnp.stack([slots, rotations]).astype(jnp.bfloat16)
    meta = jnp.pad(meta, ((0, 14), (0, pix_width - part_rows)))
    own = jnp.concatenate([particles, meta], axis=0)
    side = lax.ppermute(own, "tmpl", core_swap)
    across = lax.ppermute(own, "tmpl", y_swap)
    corner = lax.ppermute(across, "tmpl", core_swap)
    quads = [own, side, across, corner]
    slab_slots = jnp.stack([b[part_rows, :part_rows] for b in quads]).astype(jnp.int32)
    slab_rots = jnp.stack([b[part_rows + 1, :part_rows] for b in quads]).astype(jnp.int32)
    slab_target = (slab_slots // CAPACITY * rot_count + slab_rots).reshape(-1)

    per_owner = local_classes * CAPACITY
    piece = SLAB * per_owner
    near, far = (0, 1, 2, -1), (0, 4, 8, -4)
    shifts = jnp.array([[a + b for a in near] for b in far]).reshape(-1, 1, 1)
    owner_z = (level + shifts + depth) % depth
    place_slot = (owner_z * SLAB + quad) * per_owner + lax.broadcasted_iota(
        jnp.int32, (1, 1, per_owner), 2
    )
    place_slot = jnp.broadcast_to(place_slot, (depth, SLAB, per_owner))
    place = place_slot[:, :, :, None, None] == slab_slots[None, None, None]
    quad_of = lax.broadcasted_iota(jnp.int32, (1, SLAB, 1, SLAB, 1), 1)
    quad_in = lax.broadcasted_iota(jnp.int32, (1, SLAB, 1, SLAB, 1), 3)
    place = (place & (quad_of == quad_in)).astype(jnp.bfloat16)
    place = place.reshape(slot_count, SLAB * part_rows)
    slab = jnp.concatenate([b[:part_rows] for b in quads], axis=0)
    with jax.named_scope("place"):
        outgoing = jnp.dot(place, slab, preferred_element_type=jnp.float32).astype(jnp.bfloat16)
    outgoing = outgoing.reshape(len(far), len(near), piece, pix_width)
    landed = [outgoing[0]]
    for k in range(1, len(far)):
        with jax.named_scope(f"bulk_far_{k}"):
            landed.append(along(outgoing[k], far[k]))
    incoming = [jnp.concatenate([x[0] for x in landed], axis=0)]
    for k in range(1, len(near)):
        with jax.named_scope(f"bulk_near_{k}"):
            incoming.append(along(jnp.concatenate([x[k] for x in landed], axis=0), near[k]))
    incoming = jnp.concatenate(incoming, axis=0)
    arrival_z = jnp.array([[-(a + b) for b in far] for a in near]).reshape(-1)
    arrival_z = (level + arrival_z + depth) % depth

    with jax.named_scope("correlate"):
        scores = correlate(bundles, quads, part_rows)
    panel_rows = scores.shape[0]
    share = panel_rows // doms
    pieces = scores.reshape(doms, share, SLAB * part_rows)
    pieces = lax.all_to_all(pieces, "dom", split_axis=0, concat_axis=0, tiled=True)
    summed = jnp.sum(pieces, axis=0)

    inner = lax.broadcasted_iota(jnp.int32, (panel_rows,), 0) % block_rows
    source_z = (level + jnp.repeat(jnp.array(offsets), block_rows) + depth) % depth
    source = source_z * SLAB + quad
    columns = (source * local_classes + inner % local_classes) * rot_count + inner // local_classes
    my_columns = lax.dynamic_slice(columns, (dom_id * share,), (share,))

    hit = my_columns[:, None] == slab_target[None, :]
    picked = jnp.sum(jnp.where(hit, summed, 0.0), axis=0)
    square = jnp.sum(summed * summed, axis=0)
    vectors = jnp.stack([square, picked]).reshape(2, SLAB, part_rows)

    group = SLAB * doms
    spread = jnp.broadcast_to(vectors[None], (group, 2, SLAB, part_rows))
    groups = [
        [index_of(z, q) * doms + d for q in range(SLAB) for d in range(doms)] for z in range(depth)
    ]
    gathered = lax.all_to_all(
        spread, ("tmpl", "dom"), split_axis=0, concat_axis=0, tiled=True, axis_index_groups=groups
    )
    gathered = jnp.sum(gathered.reshape(SLAB, doms, 2, SLAB, part_rows), axis=1)
    totals4 = jnp.stack(
        [sum(gathered[s, :, s ^ g] for s in range(SLAB)) for g in range(SLAB)], axis=1
    )
    def canonical(x):
        y = jnp.where(core == 1, jnp.stack([x[1], x[0], x[3], x[2]]), x)
        return jnp.where(quad >= 2, jnp.stack([y[2], y[3], y[0], y[1]]), y)

    slab_weights = (totals4[1] * totals4[1] / (totals4[0] / column_count + eps)).astype(
        jnp.bfloat16
    )
    quad_iota = lax.broadcasted_iota(jnp.int32, (SLAB, 1), 0)
    weights = jnp.sum(
        jnp.where(quad_iota == quad, slab_weights.astype(jnp.float32), 0.0), axis=0
    ).astype(jnp.bfloat16)

    local_weights = canonical(slab_weights.astype(jnp.float32)).astype(jnp.bfloat16)
    z_slots = depth * per_owner
    z_iota = lax.broadcasted_iota(jnp.int32, (1, 1, z_slots), 2)
    wanted = (z_iota // per_owner * SLAB + quad) * per_owner + z_iota % per_owner
    at_slot = (slab_slots[:, :, None] == wanted).astype(jnp.bfloat16)
    values = jnp.stack([local_weights, slab_rots.astype(jnp.bfloat16)], axis=1)
    placed = jnp.einsum(
        "gvn,gns->gvs", values, at_slot, preferred_element_type=jnp.float32
    ).astype(jnp.bfloat16)
    placed = placed.reshape(SLAB, 2, depth, per_owner).transpose(2, 1, 0, 3)
    placed = placed.reshape(depth, 2, SLAB * per_owner)
    z_groups = [[index_of(z, q) for z in range(depth)] for q in range(SLAB)]
    arrived = lax.all_to_all(
        placed, "tmpl", split_axis=0, concat_axis=0, tiled=True, axis_index_groups=z_groups
    )
    source_hit = arrival_z[:, None] == lax.broadcasted_iota(jnp.int32, (depth, depth), 1)
    arrived = arrived.reshape(depth, 2 * piece)
    arrived = jnp.dot(
        source_hit.astype(jnp.bfloat16), arrived, preferred_element_type=jnp.float32
    ).reshape(depth, 2, SLAB, per_owner)
    slot_weights = arrived[:, 0].reshape(1, slot_count).astype(jnp.bfloat16)
    slot_rots = arrived[:, 1].reshape(1, slot_count).astype(jnp.int32)

    row = lax.broadcasted_iota(jnp.int32, (block_rows, slot_count), 0)
    slot = lax.broadcasted_iota(jnp.int32, (block_rows, slot_count), 1)
    match = (row % local_classes == slot % per_owner // CAPACITY) & (
        row // local_classes == slot_rots
    )
    matrix = jnp.where(match, slot_weights, jnp.zeros((), jnp.bfloat16))
    sums = jnp.dot(matrix, incoming, preferred_element_type=jnp.float32)
    totals = jnp.sum(matrix.astype(jnp.float32), axis=1, keepdims=True)
    means = sums / jnp.maximum(totals, 1.0)
    class_means = means.reshape(rot_count, local_classes, pix_width).transpose(1, 0, 2)
    return (class_means, weights)


def solution(mesh):
    return jax.shard_map(
        body,
        mesh=mesh,
        in_specs=(P("tmpl", "dom"), P("tmpl", None, "dom"), P("tmpl", None), P("tmpl")),
        out_specs=(P("tmpl", None, "dom"), P("tmpl")),
        check_vma=False,
    )
```

```python
import jax
import jax.numpy as jnp
from jax import lax
from jax.experimental import pallas as pl
from jax.experimental.pallas import tpu as pltpu
from jax.sharding import PartitionSpec as P

CAPACITY = 2
SLAB = 4
eps = 1e-05


BLOCK_PAD = 48
CHUNK = 4


def correlate_kernel(bundle_sizes, part_rows, *refs):
    bundles = refs[: len(bundle_sizes)]
    quads = refs[len(bundle_sizes) : len(bundle_sizes) + SLAB]
    out, slab, panel = refs[len(bundle_sizes) + SLAB :]
    rows = bundles[0].shape[1]
    blocks = [(ref, i) for ref, size in zip(bundles, bundle_sizes) for i in range(size)]
    for i in range(SLAB):
        slab[part_rows * i : part_rows * (i + 1), :] = quads[i][:part_rows, :]
    pad = jnp.zeros((BLOCK_PAD - rows, slab.shape[1]), jnp.bfloat16)
    for j in range(0, len(blocks), CHUNK):
        for i in range(CHUNK):
            ref, k = blocks[j + i]
            panel[BLOCK_PAD * i : BLOCK_PAD * (i + 1), :] = jnp.concatenate([ref[k], pad], axis=0)
        scores = lax.dot_general(
            panel[...], slab[...], (((1,), (1,)), ((), ())), preferred_element_type=jnp.float32
        )
        kept = [scores[BLOCK_PAD * i : BLOCK_PAD * i + rows] for i in range(CHUNK)]
        out[rows * j : rows * (j + CHUNK), :] = jnp.concatenate(kept, axis=0)


def correlate(bundles, quads, part_rows):
    sizes = [b.shape[0] for b in bundles]
    _, rows, width = bundles[0].shape
    count = sum(sizes)
    vmem = pl.BlockSpec(memory_space=pltpu.VMEM)

    def kernel(*refs):
        correlate_kernel(sizes, part_rows, *refs)

    return pl.pallas_call(
        kernel,
        out_shape=jax.ShapeDtypeStruct((count * rows, SLAB * part_rows), jnp.float32),
        in_specs=[vmem] * (len(sizes) + SLAB),
        out_specs=vmem,
        scratch_shapes=[
            pltpu.VMEM((SLAB * part_rows, width), jnp.bfloat16),
            pltpu.VMEM((CHUNK * BLOCK_PAD, width), jnp.bfloat16),
        ],
        cost_estimate=pl.CostEstimate(
            flops=2 * count * rows * width * SLAB * part_rows,
            bytes_accessed=(count * rows + SLAB * part_rows) * width * 2,
            transcendentals=0,
        ),
        name="correlate",
    )(*bundles, *quads)


def pack_rows(landed, piece):
    width = landed[0].shape[1]
    vmem = pl.BlockSpec(memory_space=pltpu.VMEM)

    def kernel(*refs):
        out = refs[-1]
        for i, ref in enumerate(refs[:-1]):
            out[piece * i : piece * (i + 1), :] = ref[piece:, :]

    return pl.pallas_call(
        kernel,
        out_shape=jax.ShapeDtypeStruct((piece * len(landed), width), jnp.bfloat16),
        in_specs=[vmem] * len(landed),
        out_specs=vmem,
        name="pack",
    )(*landed)


def average(matrix, divisor, local_classes, outgoing, opposite, landed, passed):
    piece, width = opposite.shape
    rot_count = matrix.shape[0] // local_classes
    vmem = pl.BlockSpec(memory_space=pltpu.VMEM)

    def kernel(matrix_ref, divisor_ref, *refs):
        out, rows = refs[-2:]
        for i, ref in enumerate(refs[:-3]):
            rows[piece * i : piece * (i + 1), :] = ref[:piece, :]
        rows[piece * len(refs[:-3]) :, :] = refs[-3][...]
        sums = jnp.dot(matrix_ref[...], rows[...], preferred_element_type=jnp.float32)
        means = sums / divisor_ref[...]
        for j in range(local_classes):
            out[:, j, :] = means[rot_count * j : rot_count * (j + 1)]

    own = outgoing[:piece]
    return pl.pallas_call(
        kernel,
        out_shape=jax.ShapeDtypeStruct((rot_count, local_classes, width), jnp.float32),
        in_specs=[vmem] * (5 + len(landed)),
        out_specs=vmem,
        scratch_shapes=[pltpu.VMEM((matrix.shape[1], width), jnp.bfloat16)],
        name="average",
    )(matrix, divisor, own, opposite, *landed, passed)


def body(particles, templates, classes, rotations):
    part_rows, pix_width = particles.shape
    local_classes, rot_count, _ = templates.shape
    block_rows = local_classes * rot_count
    owners = lax.axis_size("tmpl")
    doms = lax.axis_size("dom")
    depth = owners // SLAB
    column_count = owners * block_rows
    me = lax.axis_index("tmpl")
    dom_id = lax.axis_index("dom")
    quad = me % SLAB
    core = me % 2
    level = me // SLAB

    def index_of(z, q):
        return (z % depth) * SLAB + q

    everyone = [(z, q) for z in range(depth) for q in range(SLAB)]
    core_swap = [(index_of(z, q), index_of(z, q ^ 1)) for z, q in everyone]
    y_swap = [(index_of(z, q), index_of(z, q ^ 2)) for z, q in everyone]

    class_ids = classes[:, 0]
    row_iota = lax.broadcasted_iota(jnp.int32, (part_rows, part_rows), 0)
    col_iota = lax.broadcasted_iota(jnp.int32, (part_rows, part_rows), 1)
    same_class = (class_ids[:, None] == class_ids[None, :]) & (row_iota < col_iota)
    ranks = jnp.sum(same_class.astype(jnp.int32), axis=0)
    slots = class_ids * CAPACITY + ranks
    slot_count = owners * local_classes * CAPACITY

    def along(x, distance):
        hop = [(index_of(z, q), index_of(z + (distance, -distance)[q % 2], q)) for z, q in everyone]
        return lax.ppermute(x, "tmpl", hop)

    half = depth // 2
    quarter = half // 2
    own_block = templates.transpose(1, 0, 2).reshape(1, block_rows, pix_width)

    other_block = lax.ppermute(own_block, "tmpl", core_swap)
    held = {0: jnp.concatenate([own_block, other_block], axis=0)}
    held[quarter] = along(held[0], quarter)
    for k in range(1, half):
        if k != quarter:
            held[k] = along(held[k - 1], 1)
    last = along(held[half - 1][1:], 1)
    bundles = [own_block] + [held[k] for k in range(1, half)] + [last]

    meta = jnp.stack([slots, rotations]).astype(jnp.bfloat16)
    meta = jnp.pad(meta, ((0, 14), (0, pix_width - part_rows)))
    own = jnp.concatenate([particles, meta], axis=0)
    across = lax.ppermute(own, "tmpl", y_swap)
    side = lax.ppermute(own, "tmpl", core_swap)
    corner = lax.ppermute(across, "tmpl", core_swap)
    quads = [own, side, across, corner]
    slab_slots = jnp.stack([b[part_rows, :part_rows] for b in quads]).astype(jnp.int32)
    slab_rots = jnp.stack([b[part_rows + 1, :part_rows] for b in quads]).astype(jnp.int32)
    slab_target = (slab_slots // CAPACITY * rot_count + slab_rots).reshape(-1)

    per_owner = local_classes * CAPACITY
    piece = SLAB * per_owner
    way = jnp.where(core == 0, 1, -1)
    steps = [0, half] + [k for k in range(1, half) for _ in range(2)]
    flips = [0, 0] + [r for _ in range(1, half) for r in range(2)]
    owner_z = (level + way * jnp.array(steps) + depth) % depth
    owner = owner_z * SLAB + (quad ^ jnp.array(flips))
    place_slot = owner[:, None, None] * per_owner + lax.broadcasted_iota(
        jnp.int32, (1, 1, per_owner), 2
    )
    place_slot = jnp.broadcast_to(place_slot, (depth, SLAB, per_owner))
    place = place_slot[:, :, :, None, None] == slab_slots[None, None, None]
    quad_of = lax.broadcasted_iota(jnp.int32, (1, SLAB, 1, SLAB, 1), 1)
    quad_in = lax.broadcasted_iota(jnp.int32, (1, SLAB, 1, SLAB, 1), 3)
    place = (place & (quad_of == quad_in)).astype(jnp.bfloat16)
    place = place.reshape(slot_count, SLAB * part_rows)
    slab = jnp.concatenate([b[:part_rows] for b in quads], axis=0)
    outgoing = jnp.dot(place, slab, preferred_element_type=jnp.float32).astype(jnp.bfloat16)
    opposite = along(outgoing[piece : 2 * piece], half)
    landed = []
    for k in range(1, half):
        landed.append(along(outgoing[2 * piece * k : 2 * piece * (k + 1)], k))
    packed = pack_rows(landed, piece)
    passed = lax.ppermute(packed, "tmpl", core_swap)
    arrival_steps = [0, half] + list(range(1, half)) + [-k for k in range(1, half)]
    arrival_z = (level - way * jnp.array(arrival_steps) + depth) % depth

    scores = correlate(bundles, quads, part_rows)
    panel_rows = scores.shape[0]
    share = panel_rows // doms
    pieces = scores.reshape(doms, share, SLAB * part_rows)
    pieces = lax.all_to_all(pieces, "dom", split_axis=0, concat_axis=0, tiled=True)
    summed = jnp.sum(pieces, axis=0)

    inner = lax.broadcasted_iota(jnp.int32, (panel_rows,), 0) % block_rows
    hops = jnp.array([0] + [k for k in range(1, half) for _ in range(2)] + [half])
    crossed = jnp.array([0] + [0, 1] * (half - 1) + [1])
    source_z = (level - way * hops + depth) % depth
    source = jnp.repeat(source_z * SLAB + (quad ^ crossed), block_rows)
    columns = (source * local_classes + inner % local_classes) * rot_count + inner // local_classes
    my_columns = lax.dynamic_slice(columns, (dom_id * share,), (share,))

    hit = my_columns[:, None] == slab_target[None, :]
    picked = jnp.sum(jnp.where(hit, summed, 0.0), axis=0)
    square = jnp.sum(summed * summed, axis=0)
    vectors = jnp.stack([square, picked]).reshape(2, SLAB, part_rows)

    group = SLAB * doms
    spread = jnp.broadcast_to(vectors[None], (group, 2, SLAB, part_rows))
    groups = [
        [index_of(z, q) * doms + d for q in range(SLAB) for d in range(doms)] for z in range(depth)
    ]
    gathered = lax.all_to_all(
        spread,
        ("tmpl", "dom"),
        split_axis=0,
        concat_axis=0,
        tiled=True,
        axis_index_groups=groups,
    )
    gathered = jnp.sum(gathered.reshape(SLAB, doms, 2, SLAB, part_rows), axis=1)
    totals4 = jnp.stack(
        [sum(gathered[s, :, s ^ g] for s in range(SLAB)) for g in range(SLAB)], axis=1
    )

    def canonical(x):
        y = jnp.where(core == 1, jnp.stack([x[1], x[0], x[3], x[2]]), x)
        return jnp.where(quad >= 2, jnp.stack([y[2], y[3], y[0], y[1]]), y)

    slab_weights = (totals4[1] * totals4[1] / (totals4[0] / column_count + eps)).astype(
        jnp.bfloat16
    )
    quad_iota = lax.broadcasted_iota(jnp.int32, (SLAB, 1), 0)
    weights = jnp.sum(
        jnp.where(quad_iota == quad, slab_weights.astype(jnp.float32), 0.0), axis=0
    ).astype(jnp.bfloat16)

    local_weights = canonical(slab_weights.astype(jnp.float32)).astype(jnp.bfloat16)
    z_slots = depth * per_owner
    z_iota = lax.broadcasted_iota(jnp.int32, (1, 1, z_slots), 2)
    wanted = (z_iota // per_owner * SLAB + quad) * per_owner + z_iota % per_owner
    at_slot = (slab_slots[:, :, None] == wanted).astype(jnp.bfloat16)
    values = jnp.stack([local_weights, slab_rots.astype(jnp.bfloat16)], axis=1)
    placed = jnp.einsum(
        "gvn,gns->gvs", values, at_slot, preferred_element_type=jnp.float32
    ).astype(jnp.bfloat16)
    placed = placed.reshape(SLAB, 2, depth, per_owner).transpose(2, 1, 0, 3)
    placed = placed.reshape(depth, 2, SLAB * per_owner)
    z_groups = [[index_of(z, q) for z in range(depth)] for q in range(SLAB)]
    arrived = lax.all_to_all(
        placed, "tmpl", split_axis=0, concat_axis=0, tiled=True, axis_index_groups=z_groups
    )
    source_hit = arrival_z[:, None] == lax.broadcasted_iota(jnp.int32, (depth, depth), 1)
    arrived = arrived.reshape(depth, 2 * piece)
    arrived = jnp.dot(
        source_hit.astype(jnp.bfloat16), arrived, preferred_element_type=jnp.float32
    ).reshape(depth, 2, SLAB, per_owner)
    crossed_pairs = jnp.stack([arrived[:, :, i ^ 1] for i in range(SLAB)], axis=2)
    arrived = jnp.concatenate([arrived[: half + 1], crossed_pairs[half + 1 :]], axis=0)
    slot_weights = arrived[:, 0].reshape(1, slot_count).astype(jnp.bfloat16)
    slot_rots = arrived[:, 1].reshape(1, slot_count).astype(jnp.int32)

    row = lax.broadcasted_iota(jnp.int32, (block_rows, slot_count), 0)
    slot = lax.broadcasted_iota(jnp.int32, (block_rows, slot_count), 1)
    match = (row // rot_count == slot % per_owner // CAPACITY) & (row % rot_count == slot_rots)
    matrix = jnp.where(match, slot_weights, jnp.zeros((), jnp.bfloat16))
    totals = jnp.sum(matrix.astype(jnp.float32), axis=1, keepdims=True)
    divisor = jnp.maximum(totals, 1.0)
    means = average(matrix, divisor, local_classes, outgoing, opposite, landed, passed)
    class_means = means.transpose(1, 0, 2)
    return (class_means, weights)


def solution(mesh):
    return jax.shard_map(
        body,
        mesh=mesh,
        in_specs=(P("tmpl", "dom"), P("tmpl", None, "dom"), P("tmpl", None), P("tmpl")),
        out_specs=(P("tmpl", None, "dom"), P("tmpl")),
        check_vma=False,
    )
```

```python
import jax
import jax.numpy as jnp
from jax import lax
from jax.experimental import pallas as pl
from jax.experimental.pallas import tpu as pltpu
from jax.sharding import PartitionSpec as P

CAPACITY = 2
SLAB = 4
eps = 1e-05


BLOCK_PAD = 48
CHUNK = 16


def correlate_kernel(bundle_sizes, part_rows, *refs):
    bundles = refs[: len(bundle_sizes)]
    quads = refs[len(bundle_sizes) : len(bundle_sizes) + SLAB]
    out, slab, panel = refs[len(bundle_sizes) + SLAB :]
    rows = bundles[0].shape[1]
    blocks = [(ref, i) for ref, size in zip(bundles, bundle_sizes) for i in range(size)]
    for i in range(SLAB):
        slab[part_rows * i : part_rows * (i + 1), :] = quads[i][:part_rows, :]
    pad = jnp.zeros((BLOCK_PAD - rows, slab.shape[1]), jnp.bfloat16)
    for j in range(0, len(blocks), CHUNK):
        for i in range(CHUNK):
            ref, k = blocks[j + i]
            panel[BLOCK_PAD * i : BLOCK_PAD * (i + 1), :] = jnp.concatenate([ref[k], pad], axis=0)
        scores = lax.dot_general(
            panel[...], slab[...], (((1,), (1,)), ((), ())), preferred_element_type=jnp.float32
        )
        kept = [scores[BLOCK_PAD * i : BLOCK_PAD * i + rows] for i in range(CHUNK)]
        out[rows * j : rows * (j + CHUNK), :] = jnp.concatenate(kept, axis=0)


def correlate(bundles, quads, part_rows):
    sizes = [b.shape[0] for b in bundles]
    _, rows, width = bundles[0].shape
    count = sum(sizes)
    vmem = pl.BlockSpec(memory_space=pltpu.VMEM)

    def kernel(*refs):
        correlate_kernel(sizes, part_rows, *refs)

    return pl.pallas_call(
        kernel,
        out_shape=jax.ShapeDtypeStruct((count * rows, SLAB * part_rows), jnp.float32),
        in_specs=[vmem] * (len(sizes) + SLAB),
        out_specs=vmem,
        scratch_shapes=[
            pltpu.VMEM((SLAB * part_rows, width), jnp.bfloat16),
            pltpu.VMEM((CHUNK * BLOCK_PAD, width), jnp.bfloat16),
        ],
        cost_estimate=pl.CostEstimate(
            flops=2 * count * rows * width * SLAB * part_rows,
            bytes_accessed=(count * rows + SLAB * part_rows) * width * 2,
            transcendentals=0,
        ),
        name="correlate",
    )(*bundles, *quads)


def pack_rows(landed, piece):
    width = landed[0].shape[1]
    vmem = pl.BlockSpec(memory_space=pltpu.VMEM)

    def kernel(*refs):
        out = refs[-1]
        for i, ref in enumerate(refs[:-1]):
            out[piece * i : piece * (i + 1), :] = ref[piece:, :]

    return pl.pallas_call(
        kernel,
        out_shape=jax.ShapeDtypeStruct((piece * len(landed), width), jnp.bfloat16),
        in_specs=[vmem] * len(landed),
        out_specs=vmem,
        name="pack",
    )(*landed)


def average(matrix, local_classes, outgoing, opposite, landed, passed):
    piece, width = opposite.shape
    rot_count = matrix.shape[0] // local_classes
    vmem = pl.BlockSpec(memory_space=pltpu.VMEM)

    def kernel(matrix_ref, *refs):
        out, rows = refs[-2:]
        for i, ref in enumerate(refs[:-3]):
            rows[piece * i : piece * (i + 1), :] = ref[:piece, :]
        rows[piece * len(refs[:-3]) :, :] = refs[-3][...]
        sums = jnp.dot(matrix_ref[...], rows[...], preferred_element_type=jnp.float32)
        totals = jnp.sum(matrix_ref[...].astype(jnp.float32), axis=1, keepdims=True)
        means = sums / jnp.maximum(totals, 1.0)
        for j in range(local_classes):
            out[:, j, :] = means[rot_count * j : rot_count * (j + 1)]

    own = outgoing[:piece]
    return pl.pallas_call(
        kernel,
        out_shape=jax.ShapeDtypeStruct((rot_count, local_classes, width), jnp.float32),
        in_specs=[vmem] * (4 + len(landed)),
        out_specs=vmem,
        scratch_shapes=[pltpu.VMEM((matrix.shape[1], width), jnp.bfloat16)],
        name="average",
    )(matrix, own, opposite, *landed, passed)


def body(particles, templates, classes, rotations):
    part_rows, pix_width = particles.shape
    local_classes, rot_count, _ = templates.shape
    block_rows = local_classes * rot_count
    owners = lax.axis_size("tmpl")
    doms = lax.axis_size("dom")
    depth = owners // SLAB
    column_count = owners * block_rows
    me = lax.axis_index("tmpl")
    dom_id = lax.axis_index("dom")
    quad = me % SLAB
    core = me % 2
    level = me // SLAB

    def index_of(z, q):
        return (z % depth) * SLAB + q

    everyone = [(z, q) for z in range(depth) for q in range(SLAB)]
    core_swap = [(index_of(z, q), index_of(z, q ^ 1)) for z, q in everyone]
    y_swap = [(index_of(z, q), index_of(z, q ^ 2)) for z, q in everyone]

    class_ids = classes[:, 0]
    row_iota = lax.broadcasted_iota(jnp.int32, (part_rows, part_rows), 0)
    col_iota = lax.broadcasted_iota(jnp.int32, (part_rows, part_rows), 1)
    same_class = (class_ids[:, None] == class_ids[None, :]) & (row_iota < col_iota)
    ranks = jnp.sum(same_class.astype(jnp.int32), axis=0)
    slots = class_ids * CAPACITY + ranks
    slot_count = owners * local_classes * CAPACITY

    def along(x, distance):
        hop = [(index_of(z, q), index_of(z + (distance, -distance)[q % 2], q)) for z, q in everyone]
        return lax.ppermute(x, "tmpl", hop)

    half = depth // 2
    leap = half // 2 + 1
    own_block = templates.transpose(1, 0, 2).reshape(1, block_rows, pix_width)

    other_block = lax.ppermute(own_block, "tmpl", core_swap)
    held = {0: jnp.concatenate([own_block, other_block], axis=0)}
    held[leap] = along(held[0], leap)
    for k in range(1, half):
        if k != leap:
            held[k] = along(held[k - 1], 1)
    last = along(held[half - 1][1:], 1)
    bundles = [own_block] + [held[k] for k in range(1, half)] + [last]

    meta = jnp.stack([slots, rotations]).astype(jnp.bfloat16)
    meta = jnp.pad(meta, ((0, 14), (0, pix_width - part_rows)))
    own = jnp.concatenate([particles, meta], axis=0)
    across = lax.ppermute(own, "tmpl", y_swap)
    side = lax.ppermute(own, "tmpl", core_swap)
    corner = lax.ppermute(across, "tmpl", core_swap)
    quads = [own, side, across, corner]
    slab_slots = jnp.stack([b[part_rows, :part_rows] for b in quads]).astype(jnp.int32)
    slab_rots = jnp.stack([b[part_rows + 1, :part_rows] for b in quads]).astype(jnp.int32)
    slab_target = (slab_slots // CAPACITY * rot_count + slab_rots).reshape(-1)

    per_owner = local_classes * CAPACITY
    piece = SLAB * per_owner
    way = jnp.where(core == 0, 1, -1)
    steps = [0, half] + [k for k in range(1, half) for _ in range(2)]
    flips = [0, 0] + [r for _ in range(1, half) for r in range(2)]
    owner_z = (level + way * jnp.array(steps) + depth) % depth
    owner = owner_z * SLAB + (quad ^ jnp.array(flips))
    place_slot = owner[:, None, None] * per_owner + lax.broadcasted_iota(
        jnp.int32, (1, 1, per_owner), 2
    )
    place_slot = jnp.broadcast_to(place_slot, (depth, SLAB, per_owner))
    place = place_slot[:, :, :, None, None] == slab_slots[None, None, None]
    quad_of = lax.broadcasted_iota(jnp.int32, (1, SLAB, 1, SLAB, 1), 1)
    quad_in = lax.broadcasted_iota(jnp.int32, (1, SLAB, 1, SLAB, 1), 3)
    place = (place & (quad_of == quad_in)).astype(jnp.bfloat16)
    place = place.reshape(slot_count, SLAB * part_rows)
    slab = jnp.concatenate([b[:part_rows] for b in quads], axis=0)
    outgoing = jnp.dot(place, slab, preferred_element_type=jnp.float32).astype(jnp.bfloat16)
    opposite = along(outgoing[piece : 2 * piece], half)
    landed = []
    for k in range(1, half):
        landed.append(along(outgoing[2 * piece * k : 2 * piece * (k + 1)], k))
    packed = pack_rows(landed, piece)
    passed = lax.ppermute(packed, "tmpl", core_swap)
    arrival_steps = [0, half] + list(range(1, half)) + [-k for k in range(1, half)]
    arrival_z = (level - way * jnp.array(arrival_steps) + depth) % depth

    scores = correlate(bundles, quads, part_rows)
    panel_rows = scores.shape[0]
    share = panel_rows // doms
    pieces = scores.reshape(doms, share, SLAB * part_rows)
    pieces = lax.all_to_all(pieces, "dom", split_axis=0, concat_axis=0, tiled=True)
    summed = jnp.sum(pieces, axis=0)

    inner = lax.broadcasted_iota(jnp.int32, (panel_rows,), 0) % block_rows
    hops = jnp.array([0] + [k for k in range(1, half) for _ in range(2)] + [half])
    crossed = jnp.array([0] + [0, 1] * (half - 1) + [1])
    source_z = (level - way * hops + depth) % depth
    source = jnp.repeat(source_z * SLAB + (quad ^ crossed), block_rows)
    columns = (source * local_classes + inner % local_classes) * rot_count + inner // local_classes
    my_columns = lax.dynamic_slice(columns, (dom_id * share,), (share,))

    hit = my_columns[:, None] == slab_target[None, :]
    picked = jnp.sum(jnp.where(hit, summed, 0.0), axis=0)
    square = jnp.sum(summed * summed, axis=0)
    vectors = jnp.stack([square, picked]).reshape(2, SLAB, part_rows)

    group = SLAB * doms
    spread = jnp.broadcast_to(vectors[None], (group, 2, SLAB, part_rows))
    groups = [
        [index_of(z, q) * doms + d for q in range(SLAB) for d in range(doms)] for z in range(depth)
    ]
    gathered = lax.all_to_all(
        spread,
        ("tmpl", "dom"),
        split_axis=0,
        concat_axis=0,
        tiled=True,
        axis_index_groups=groups,
    )
    gathered = jnp.sum(gathered.reshape(SLAB, doms, 2, SLAB, part_rows), axis=1)
    totals4 = jnp.stack(
        [sum(gathered[s, :, s ^ g] for s in range(SLAB)) for g in range(SLAB)], axis=1
    )

    def canonical(x):
        y = jnp.where(core == 1, jnp.stack([x[1], x[0], x[3], x[2]]), x)
        return jnp.where(quad >= 2, jnp.stack([y[2], y[3], y[0], y[1]]), y)

    slab_weights = (totals4[1] * totals4[1] / (totals4[0] / column_count + eps)).astype(
        jnp.bfloat16
    )
    quad_iota = lax.broadcasted_iota(jnp.int32, (SLAB, 1), 0)
    weights = jnp.sum(
        jnp.where(quad_iota == quad, slab_weights.astype(jnp.float32), 0.0), axis=0
    ).astype(jnp.bfloat16)

    local_weights = canonical(slab_weights.astype(jnp.float32)).astype(jnp.bfloat16)
    z_slots = depth * per_owner
    z_iota = lax.broadcasted_iota(jnp.int32, (1, 1, z_slots), 2)
    wanted = (z_iota // per_owner * SLAB + quad) * per_owner + z_iota % per_owner
    at_slot = (slab_slots[:, :, None] == wanted).astype(jnp.bfloat16)
    values = jnp.stack([local_weights, slab_rots.astype(jnp.bfloat16)], axis=1)
    placed = jnp.einsum(
        "gvn,gns->gvs", values, at_slot, preferred_element_type=jnp.float32
    ).astype(jnp.bfloat16)
    placed = placed.reshape(SLAB, 2, depth, per_owner).transpose(2, 1, 0, 3)
    placed = placed.reshape(depth, 2, SLAB * per_owner)
    z_groups = [[index_of(z, q) for z in range(depth)] for q in range(SLAB)]
    arrived = lax.all_to_all(
        placed, "tmpl", split_axis=0, concat_axis=0, tiled=True, axis_index_groups=z_groups
    )
    source_hit = arrival_z[:, None] == lax.broadcasted_iota(jnp.int32, (depth, depth), 1)
    arrived = arrived.reshape(depth, 2 * piece)
    arrived = jnp.dot(
        source_hit.astype(jnp.bfloat16), arrived, preferred_element_type=jnp.float32
    ).reshape(depth, 2, SLAB, per_owner)
    crossed_pairs = jnp.stack([arrived[:, :, i ^ 1] for i in range(SLAB)], axis=2)
    arrived = jnp.concatenate([arrived[: half + 1], crossed_pairs[half + 1 :]], axis=0)
    slot_weights = arrived[:, 0].reshape(1, slot_count).astype(jnp.bfloat16)
    slot_rots = arrived[:, 1].reshape(1, slot_count).astype(jnp.int32)

    row = lax.broadcasted_iota(jnp.int32, (block_rows, slot_count), 0)
    slot = lax.broadcasted_iota(jnp.int32, (block_rows, slot_count), 1)
    match = (row // rot_count == slot % per_owner // CAPACITY) & (row % rot_count == slot_rots)
    matrix = jnp.where(match, slot_weights, jnp.zeros((), jnp.bfloat16))
    means = average(matrix, local_classes, outgoing, opposite, landed, passed)
    class_means = means.transpose(1, 0, 2)
    return (class_means, weights)


def solution(mesh):
    return jax.shard_map(
        body,
        mesh=mesh,
        in_specs=(P("tmpl", "dom"), P("tmpl", None, "dom"), P("tmpl", None), P("tmpl")),
        out_specs=(P("tmpl", None, "dom"), P("tmpl")),
        check_vma=False,
    )
```

```python
import jax
import jax.numpy as jnp
from jax import lax
from jax.experimental import pallas as pl
from jax.experimental.pallas import tpu as pltpu
from jax.sharding import PartitionSpec as P

CAPACITY = 2
SLAB = 4
eps = 1e-05


BLOCK_PAD = 48
CHUNK = 16


def correlate_kernel(bundle_sizes, part_rows, *refs):
    bundles = refs[: len(bundle_sizes)]
    quads = refs[len(bundle_sizes) : len(bundle_sizes) + SLAB]
    out, slab, panel = refs[len(bundle_sizes) + SLAB :]
    rows = bundles[0].shape[1]
    blocks = [(ref, i) for ref, size in zip(bundles, bundle_sizes) for i in range(size)]
    for i in range(SLAB):
        slab[part_rows * i : part_rows * (i + 1), :] = quads[i][:part_rows, :]
    pad = jnp.zeros((BLOCK_PAD - rows, slab.shape[1]), jnp.bfloat16)
    for j in range(0, len(blocks), CHUNK):
        for i in range(CHUNK):
            ref, k = blocks[j + i]
            panel[BLOCK_PAD * i : BLOCK_PAD * (i + 1), :] = jnp.concatenate([ref[k], pad], axis=0)
        scores = lax.dot_general(
            panel[...], slab[...], (((1,), (1,)), ((), ())), preferred_element_type=jnp.float32
        )
        kept = [scores[BLOCK_PAD * i : BLOCK_PAD * i + rows] for i in range(CHUNK)]
        out[rows * j : rows * (j + CHUNK), :] = jnp.concatenate(kept, axis=0)


def correlate(bundles, quads, part_rows):
    sizes = [b.shape[0] for b in bundles]
    _, rows, width = bundles[0].shape
    count = sum(sizes)
    vmem = pl.BlockSpec(memory_space=pltpu.VMEM)

    def kernel(*refs):
        correlate_kernel(sizes, part_rows, *refs)

    return pl.pallas_call(
        kernel,
        out_shape=jax.ShapeDtypeStruct((count * rows, SLAB * part_rows), jnp.float32),
        in_specs=[vmem] * (len(sizes) + SLAB),
        out_specs=vmem,
        scratch_shapes=[
            pltpu.VMEM((SLAB * part_rows, width), jnp.bfloat16),
            pltpu.VMEM((CHUNK * BLOCK_PAD, width), jnp.bfloat16),
        ],
        cost_estimate=pl.CostEstimate(
            flops=2 * count * rows * width * SLAB * part_rows,
            bytes_accessed=(count * rows + SLAB * part_rows) * width * 2,
            transcendentals=0,
        ),
        name="correlate",
    )(*bundles, *quads)


def pack_rows(landed, piece):
    width = landed[0].shape[1]
    vmem = pl.BlockSpec(memory_space=pltpu.VMEM)

    def kernel(*refs):
        out = refs[-1]
        for i, ref in enumerate(refs[:-1]):
            out[piece * i : piece * (i + 1), :] = ref[piece:, :]

    return pl.pallas_call(
        kernel,
        out_shape=jax.ShapeDtypeStruct((piece * len(landed), width), jnp.bfloat16),
        in_specs=[vmem] * len(landed),
        out_specs=vmem,
        compiler_params=pltpu.CompilerParams(vmem_limit_bytes=16 * 2**20),
        name="pack",
    )(*landed)


def average(matrix, local_classes, outgoing, opposite, landed, passed):
    piece, width = opposite.shape
    rot_count = matrix.shape[0] // local_classes
    vmem = pl.BlockSpec(memory_space=pltpu.VMEM)

    def kernel(matrix_ref, *refs):
        out, rows = refs[-2:]
        for i, ref in enumerate(refs[:-3]):
            rows[piece * i : piece * (i + 1), :] = ref[:piece, :]
        rows[piece * len(refs[:-3]) :, :] = refs[-3][...]
        sums = jnp.dot(matrix_ref[...], rows[...], preferred_element_type=jnp.float32)
        totals = jnp.sum(matrix_ref[...].astype(jnp.float32), axis=1, keepdims=True)
        means = sums / jnp.maximum(totals, 1.0)
        for j in range(local_classes):
            out[:, j, :] = means[rot_count * j : rot_count * (j + 1)]

    own = outgoing[:piece]
    return pl.pallas_call(
        kernel,
        out_shape=jax.ShapeDtypeStruct((rot_count, local_classes, width), jnp.float32),
        in_specs=[vmem] * (4 + len(landed)),
        out_specs=vmem,
        scratch_shapes=[pltpu.VMEM((matrix.shape[1], width), jnp.bfloat16)],
        compiler_params=pltpu.CompilerParams(vmem_limit_bytes=16 * 2**20),
        name="average",
    )(matrix, own, opposite, *landed, passed)


def body(particles, templates, classes, rotations):
    part_rows, pix_width = particles.shape
    local_classes, rot_count, _ = templates.shape
    block_rows = local_classes * rot_count
    owners = lax.axis_size("tmpl")
    doms = lax.axis_size("dom")
    depth = owners // SLAB
    column_count = owners * block_rows
    me = lax.axis_index("tmpl")
    dom_id = lax.axis_index("dom")
    quad = me % SLAB
    core = me % 2
    level = me // SLAB

    def index_of(z, q):
        return (z % depth) * SLAB + q

    everyone = [(z, q) for z in range(depth) for q in range(SLAB)]
    core_swap = [(index_of(z, q), index_of(z, q ^ 1)) for z, q in everyone]
    y_swap = [(index_of(z, q), index_of(z, q ^ 2)) for z, q in everyone]

    class_ids = classes[:, 0]
    row_iota = lax.broadcasted_iota(jnp.int32, (part_rows, part_rows), 0)
    col_iota = lax.broadcasted_iota(jnp.int32, (part_rows, part_rows), 1)
    same_class = (class_ids[:, None] == class_ids[None, :]) & (row_iota < col_iota)
    ranks = jnp.sum(same_class.astype(jnp.int32), axis=0)
    slots = class_ids * CAPACITY + ranks
    slot_count = owners * local_classes * CAPACITY

    def along(x, distance):
        hop = [(index_of(z, q), index_of(z + (distance, -distance)[q % 2], q)) for z, q in everyone]
        return lax.ppermute(x, "tmpl", hop)

    half = depth // 2
    leap = half // 2 + 1
    own_block = templates.transpose(1, 0, 2).reshape(1, block_rows, pix_width)

    other_block = lax.ppermute(own_block, "tmpl", core_swap)
    held = {0: jnp.concatenate([own_block, other_block], axis=0)}
    cross = [
        (index_of(z, q), index_of(z + (-leap, leap)[q % 2], q ^ 1)) for z, q in everyone
    ]
    leapt = along(own_block, leap)
    crossed_leap = lax.ppermute(own_block, "tmpl", cross)
    held[leap] = jnp.concatenate([leapt, crossed_leap], axis=0)
    for k in range(1, half):
        if k != leap:
            held[k] = along(held[k - 1], 1)
    last = along(held[half - 1][1:], 1)
    bundles = [own_block] + [held[k] for k in range(1, half)] + [last]

    meta = jnp.stack([slots, rotations]).astype(jnp.bfloat16)
    meta = jnp.pad(meta, ((0, 14), (0, pix_width - part_rows)))
    own = jnp.concatenate([particles, meta], axis=0)
    across = lax.ppermute(own, "tmpl", y_swap)
    side = lax.ppermute(own, "tmpl", core_swap)
    corner = lax.ppermute(across, "tmpl", core_swap)
    quads = [own, side, across, corner]
    slab_slots = jnp.stack([b[part_rows, :part_rows] for b in quads]).astype(jnp.int32)
    slab_rots = jnp.stack([b[part_rows + 1, :part_rows] for b in quads]).astype(jnp.int32)
    slab_target = (slab_slots // CAPACITY * rot_count + slab_rots).reshape(-1)

    per_owner = local_classes * CAPACITY
    piece = SLAB * per_owner
    way = jnp.where(core == 0, 1, -1)
    steps = [0, half] + [k for k in range(1, half) for _ in range(2)]
    flips = [0, 0] + [r for _ in range(1, half) for r in range(2)]
    owner_z = (level + way * jnp.array(steps) + depth) % depth
    owner = owner_z * SLAB + (quad ^ jnp.array(flips))
    place_slot = owner[:, None, None] * per_owner + lax.broadcasted_iota(
        jnp.int32, (1, 1, per_owner), 2
    )
    place_slot = jnp.broadcast_to(place_slot, (depth, SLAB, per_owner))
    place = place_slot[:, :, :, None, None] == slab_slots[None, None, None]
    quad_of = lax.broadcasted_iota(jnp.int32, (1, SLAB, 1, SLAB, 1), 1)
    quad_in = lax.broadcasted_iota(jnp.int32, (1, SLAB, 1, SLAB, 1), 3)
    place = (place & (quad_of == quad_in)).astype(jnp.bfloat16)
    place = place.reshape(slot_count, SLAB * part_rows)
    slab = jnp.concatenate([b[:part_rows] for b in quads], axis=0)
    outgoing = jnp.dot(place, slab, preferred_element_type=jnp.float32).astype(jnp.bfloat16)
    opposite = along(outgoing[piece : 2 * piece], half)
    landed = []
    for k in range(1, half):
        landed.append(along(outgoing[2 * piece * k : 2 * piece * (k + 1)], k))
    packed = pack_rows(landed, piece)
    passed = lax.ppermute(packed, "tmpl", core_swap)
    arrival_steps = [0, half] + list(range(1, half)) + [-k for k in range(1, half)]
    arrival_z = (level - way * jnp.array(arrival_steps) + depth) % depth

    scores = correlate(bundles, quads, part_rows)
    panel_rows = scores.shape[0]
    share = panel_rows // doms
    pieces = scores.reshape(doms, share, SLAB * part_rows)
    pieces = lax.all_to_all(pieces, "dom", split_axis=0, concat_axis=0, tiled=True)
    summed = jnp.sum(pieces, axis=0)

    inner = lax.broadcasted_iota(jnp.int32, (panel_rows,), 0) % block_rows
    hops = jnp.array([0] + [k for k in range(1, half) for _ in range(2)] + [half])
    crossed = jnp.array([0] + [0, 1] * (half - 1) + [1])
    source_z = (level - way * hops + depth) % depth
    source = jnp.repeat(source_z * SLAB + (quad ^ crossed), block_rows)
    columns = (source * local_classes + inner % local_classes) * rot_count + inner // local_classes
    my_columns = lax.dynamic_slice(columns, (dom_id * share,), (share,))

    hit = my_columns[:, None] == slab_target[None, :]
    picked = jnp.sum(jnp.where(hit, summed, 0.0), axis=0)
    square = jnp.sum(summed * summed, axis=0)
    vectors = jnp.stack([square, picked]).reshape(2, SLAB, part_rows)

    group = SLAB * doms
    spread = jnp.broadcast_to(vectors[None], (group, 2, SLAB, part_rows))
    groups = [
        [index_of(z, q) * doms + d for q in range(SLAB) for d in range(doms)] for z in range(depth)
    ]
    gathered = lax.all_to_all(
        spread,
        ("tmpl", "dom"),
        split_axis=0,
        concat_axis=0,
        tiled=True,
        axis_index_groups=groups,
    )
    gathered = jnp.sum(gathered.reshape(SLAB, doms, 2, SLAB, part_rows), axis=1)
    totals4 = jnp.stack(
        [sum(gathered[s, :, s ^ g] for s in range(SLAB)) for g in range(SLAB)], axis=1
    )

    def canonical(x):
        y = jnp.where(core == 1, jnp.stack([x[1], x[0], x[3], x[2]]), x)
        return jnp.where(quad >= 2, jnp.stack([y[2], y[3], y[0], y[1]]), y)

    slab_weights = (totals4[1] * totals4[1] / (totals4[0] / column_count + eps)).astype(
        jnp.bfloat16
    )
    quad_iota = lax.broadcasted_iota(jnp.int32, (SLAB, 1), 0)
    weights = jnp.sum(
        jnp.where(quad_iota == quad, slab_weights.astype(jnp.float32), 0.0), axis=0
    ).astype(jnp.bfloat16)

    local_weights = canonical(slab_weights.astype(jnp.float32)).astype(jnp.bfloat16)
    z_slots = depth * per_owner
    z_iota = lax.broadcasted_iota(jnp.int32, (1, 1, z_slots), 2)
    wanted = (z_iota // per_owner * SLAB + quad) * per_owner + z_iota % per_owner
    at_slot = (slab_slots[:, :, None] == wanted).astype(jnp.bfloat16)
    values = jnp.stack([local_weights, slab_rots.astype(jnp.bfloat16)], axis=1)
    placed = jnp.einsum(
        "gvn,gns->gvs", values, at_slot, preferred_element_type=jnp.float32
    ).astype(jnp.bfloat16)
    placed = placed.reshape(SLAB, 2, depth, per_owner).transpose(2, 1, 0, 3)
    placed = placed.reshape(depth, 2, SLAB * per_owner)
    z_groups = [[index_of(z, q) for z in range(depth)] for q in range(SLAB)]
    arrived = lax.all_to_all(
        placed, "tmpl", split_axis=0, concat_axis=0, tiled=True, axis_index_groups=z_groups
    )
    source_hit = arrival_z[:, None] == lax.broadcasted_iota(jnp.int32, (depth, depth), 1)
    arrived = arrived.reshape(depth, 2 * piece)
    arrived = jnp.dot(
        source_hit.astype(jnp.bfloat16), arrived, preferred_element_type=jnp.float32
    ).reshape(depth, 2, SLAB, per_owner)
    crossed_pairs = jnp.stack([arrived[:, :, i ^ 1] for i in range(SLAB)], axis=2)
    arrived = jnp.concatenate([arrived[: half + 1], crossed_pairs[half + 1 :]], axis=0)
    slot_weights = arrived[:, 0].reshape(1, slot_count).astype(jnp.bfloat16)
    slot_rots = arrived[:, 1].reshape(1, slot_count).astype(jnp.int32)

    row = lax.broadcasted_iota(jnp.int32, (block_rows, slot_count), 0)
    slot = lax.broadcasted_iota(jnp.int32, (block_rows, slot_count), 1)
    match = (row // rot_count == slot % per_owner // CAPACITY) & (row % rot_count == slot_rots)
    matrix = jnp.where(match, slot_weights, jnp.zeros((), jnp.bfloat16))
    means = average(matrix, local_classes, outgoing, opposite, landed, passed)
    class_means = means.transpose(1, 0, 2)
    return (class_means, weights)


def solution(mesh):
    return jax.shard_map(
        body,
        mesh=mesh,
        in_specs=(P("tmpl", "dom"), P("tmpl", None, "dom"), P("tmpl", None), P("tmpl")),
        out_specs=(P("tmpl", None, "dom"), P("tmpl")),
        check_vma=False,
    )
```
